256 devices in a mesh: dp: 16 (over x, y_hi, core), tensor: 16 (over y_lo, z).
Axes of the slice: x: 4, y: 4 (y_hi: 2, y_lo: 2; y = y_hi * 2 + y_lo), z: 8, core: 2. Of those that a mesh axis runs over, the one named last changes fastest.
Arguments:
- inputs: bfloat16 [8192, 6144], P(('dp', 'tensor')), may hold values from -36 to 36
- gain: float32 [6144], replicated, may hold values from 0.25 to 1.75
- w_in: bfloat16 [6144, 12288], P(None, 'tensor'), may hold values from -0.078125 to 0.078125
- grad_act: bfloat16 [8192, 12288], P('dp', 'tensor'), may hold values from -6 to 6
- residual_gradient: bfloat16 [8192, 6144], P(('dp', 'tensor')), may hold values from -6 to 6
Outputs:
- block_input_gradient: bfloat16 [8192, 6144], P(('dp', 'tensor'))
- grad_w: float32 [6144, 12288], P('dp', 'tensor')
- scale_gradient: float32 [6144], replicated
The draws below stay inside these ranges and needn't reach their ends.
All inputs are finite; a program needn't handle non-finite values.
Results may differ from the reference program's by a relative error of at most 0.022.
Values may be sent and summed in bfloat16 or wider, within the bound.
No kernel may reach another device: no remote copies, remote signals or barrier semaphores. Data moves between devices by JAX's collectives and lax.ppermute only.
A program may use at most 128 MiB of HBM per device.

```python
import math
import jax
import jax.numpy as jnp
from jax import lax

D = 6144
FF = 12288
TOK = 512
TOKENS = 8192
N_DP = 16
N_TENSOR = 16


def draw_inputs(key, part):
    keys = jax.random.split(key, 3)
    row_scale = jnp.exp(jax.random.uniform(keys[0], (TOKENS, 1), jnp.float32, math.log(0.3), math.log(3.0)))
    col_scale = jnp.exp(jax.random.uniform(keys[1], (1, D), jnp.float32, math.log(0.3), math.log(3.0)))
    base = jax.random.truncated_normal(keys[2], -4.0, 4.0, (TOKENS, D), jnp.float32)
    values = row_scale * col_scale * base
    return jnp.clip(values, -36.0, 36.0).astype(jnp.bfloat16)


def level_of(own_key, shape, cuts, smallest, top_value):
    level, own = 1.0, jax.random.fold_in(own_key, 6)
    for axis_at, parts in cuts:
        steps = jnp.exp(jax.random.uniform(jax.random.fold_in(own, axis_at), (parts,), jnp.float32, smallest / len(cuts), top_value / len(cuts)))
        level = level * jnp.repeat(steps, shape[axis_at] // parts).reshape([-1 if axis == axis_at else 1 for axis in range(len(shape))])
    return level


def centred(stream_key, shape, deviation, limit, cuts=(), kind=jnp.bfloat16):
    result = deviation * jax.random.normal(stream_key, shape, jnp.float32)
    if cuts:
        result = result * level_of(stream_key, shape, cuts, -0.22, 0.18)
    return jnp.clip(result, -limit, limit).astype(kind)


def setup_inputs(seed: int = 0) -> dict:
    seeds = jax.random.split(jax.random.key(seed), 6)
    inputs = draw_inputs(jax.random.fold_in(seeds[5], 71), 0)
    gain = jnp.clip(1.0 + 0.15 * jax.random.normal(seeds[1], (D,), jnp.float32), 0.25, 1.75)
    w_in = centred(seeds[2], (D, FF), D ** -0.5, 0.078125, ((1, 16),))
    grad_act = centred(seeds[3], (TOKENS, FF), 1.0, 6.0, ((0, 16), (1, 16)))
    residual_gradient = centred(seeds[4], (TOKENS, D), 1.0, 6.0, ((0, 256),))
    return dict(inputs=inputs, gain=gain, w_in=w_in, grad_act=grad_act, residual_gradient=residual_gradient)


def reference(inputs, gain, w_in, grad_act, residual_gradient):
    values = inputs.astype(jnp.float32)
    centered_input = values - lax.optimization_barrier(jnp.mean(values, axis=1, keepdims=True))
    inverse_deviation = lax.rsqrt(lax.optimization_barrier(jnp.mean(centered_input * centered_input, axis=1, keepdims=True)) + 1e-06)
    standardized_input = centered_input * inverse_deviation
    normed_output = (standardized_input * gain).astype(jnp.bfloat16)
    pre = jnp.dot(normed_output, w_in, preferred_element_type=jnp.float32)
    unused, pullback = jax.vjp(jax.nn.gelu, pre)
    dpre = pullback(grad_act.astype(jnp.float32))[0].astype(jnp.bfloat16)
    width = FF // N_TENSOR

    def add_block(total, index):
        start = (index * width).astype(jnp.int32)
        cols = lax.dynamic_slice_in_dim(dpre, start, width, 1)
        rows = lax.dynamic_slice_in_dim(w_in, start, width, 1)
        part = lax.dot_general(cols, rows, (((1,), (1,)), ((), ())), preferred_element_type=jnp.float32)
        return (total + lax.optimization_barrier(part.astype(jnp.bfloat16)).astype(jnp.float32), None)
    normed_gradient, unused_b = lax.scan(add_block, jnp.zeros((TOKENS, D), jnp.float32), jnp.arange(N_TENSOR, dtype=jnp.int32))
    scale_gradient = lax.optimization_barrier(jnp.sum(normed_gradient * standardized_input, axis=0)) / N_DP
    scaled_gradient = normed_gradient * gain
    first_average = lax.optimization_barrier(jnp.mean(scaled_gradient, axis=1, keepdims=True))
    second_average = lax.optimization_barrier(jnp.mean(scaled_gradient * standardized_input, axis=1, keepdims=True))
    block_input_gradient = (residual_gradient.astype(jnp.float32) + inverse_deviation * (scaled_gradient - first_average - standardized_input * second_average)).astype(jnp.bfloat16)

    def add_replica(total, index):
        start = (index * TOK).astype(jnp.int32)
        left = lax.dynamic_slice_in_dim(normed_output, start, TOK, 0)
        right = lax.dynamic_slice_in_dim(dpre, start, TOK, 0)
        part = lax.dot_general(left, right, (((0,), (0,)), ((), ())), preferred_element_type=jnp.float32)
        return (total + lax.optimization_barrier(part.astype(jnp.bfloat16)).astype(jnp.float32), None)
    summed, unused_c = lax.scan(add_replica, jnp.zeros((D, FF), jnp.float32), jnp.arange(N_DP, dtype=jnp.int32))
    grad_w = summed / N_DP
    return (block_input_gradient, grad_w, scale_gradient)
```

```python
import jax
import jax.numpy as jnp
from jax import lax
from jax.experimental import pallas as pl
from jax.experimental.pallas import tpu as pltpu
from jax.sharding import PartitionSpec as P

F32 = jnp.float32
BF16 = jnp.bfloat16
ROWS = 32
NZ = 8
CH = 384


def ppermute(value, axis, target):
    return lax.ppermute(value, axis, [(i, target(i)) for i in range(16)])


def z_shift(step):
    return lambda i: (i // NZ) * NZ + (i + step) % NZ


def to_z(value, step):
    return ppermute(value, "tensor", z_shift(step))


def swap_y(value):
    return ppermute(value, "tensor", lambda i: i ^ 8)


def to_x(value, step):
    return ppermute(value, "dp", lambda i: (i + 4 * step) % 16)


def swap_yh(value):
    return ppermute(value, "dp", lambda i: i ^ 2)


def swap_core(value):
    return ppermute(value, "dp", lambda i: i ^ 1)


def add(*terms):
    total = terms[0].astype(F32)
    for term in terms[1:]:
        total = total + term.astype(F32)
    return total.astype(BF16)


GROUPS = (
    (("A", 0), ("A", 1), ("A", -1), ("B", 0)),
    (("A", 2), ("A", -2), ("B", 1)),
    (("A", 3), ("A", -3), ("B", 2)),
    (("B", 3), ("A", 4), ("B", -2)),
    (("B", 4), ("B", -3), ("B", -1)),
)


def gather_tokens(own):
    got = {("A", 0): own}
    got["A", 1] = to_z(own, -1)
    got["A", -1] = to_z(own, 1)
    got["B", 0] = swap_y(own)
    got["A", 2] = to_z(got["A", 1], -1)
    got["A", -2] = to_z(got["A", -1], 1)
    got["B", 1] = swap_y(got["A", 1])
    got["A", 3] = to_z(got["A", 2], -1)
    got["A", -3] = to_z(got["A", -2], 1)
    got["B", 2] = swap_y(got["A", 2])
    got["B", 3] = to_z(got["B", 2], -1)
    got["A", 4] = to_z(got["A", -3], 1)
    got["B", -2] = swap_y(got["A", -2])
    got["B", 4] = to_z(got["B", 3], -1)
    got["B", -3] = to_z(got["B", -2], 1)
    got["B", -1] = swap_y(got["A", -1])
    return got


def scatter_tokens(part):
    part = dict(part)

    def step(moves):
        arrived = [(into, move(part[key])) for key, move, into in moves]
        for into, value in arrived:
            part[into] = part[into] + (value,) if isinstance(part[into], tuple) else (part[into], value)
        for into, _ in arrived:
            if isinstance(part[into], tuple):
                part[into] = add(*part[into])

    up = lambda v: to_z(v, 1)
    down = lambda v: to_z(v, -1)
    step([(("B", 4), up, ("B", 3)), (("B", -3), down, ("B", -2)), (("B", -1), swap_y, ("A", -1))])
    step([(("B", 3), up, ("B", 2)), (("A", 4), down, ("A", -3)), (("B", -2), swap_y, ("A", -2))])
    step([(("A", 3), up, ("A", 2)), (("A", -3), down, ("A", -2)), (("B", 2), swap_y, ("A", 2))])
    step([(("A", 2), up, ("A", 1)), (("A", -2), down, ("A", -1)), (("B", 1), swap_y, ("A", 1))])
    last = [part["A", 0], up(part["A", 1]), down(part["A", -1]), swap_y(part["B", 0])]
    return last[0].astype(F32) + last[1].astype(F32) + last[2].astype(F32) + last[3].astype(F32)


def weight_kernel(order, *refs):
    n = (len(refs) - 5) // 2
    lefts, rights = refs[:n], refs[n : 2 * n]
    w_ref, unused, out_ref, sum_ref = refs[2 * n], refs[2 * n + 1], refs[2 * n + 2], refs[2 * n + 3]
    acc_ref = refs[2 * n + 4]
    total = None
    for left, right in zip(lefts, rights):
        term = lax.dot_general(
            left[...], right[...], (((0,), (0,)), ((), ())), preferred_element_type=F32
        )
        total = term if total is None else total + term
    acc_ref[...] = total
    out_ref[...] = acc_ref[...].astype(BF16)
    weighted = acc_ref[:, 0:128] * w_ref[:, 0:128].astype(F32)
    for lane in range(128, acc_ref.shape[1], 128):
        weighted = weighted + acc_ref[:, lane : lane + 128] * w_ref[:, lane : lane + 128].astype(F32)
    sum_ref[...] = weighted


def weight_terms(order, lefts, rights, w_in, sums):
    width = w_in.shape[1]
    count = order.shape[0]
    n = len(lefts)
    specs = [pl.BlockSpec((left.shape[0], CH), lambda j, o: (0, o[j])) for left in lefts]
    specs += [pl.BlockSpec((right.shape[0], width), lambda j, o: (0, 0)) for right in rights]
    specs += [pl.BlockSpec((CH, width), lambda j, o: (o[j], 0)), pl.BlockSpec(memory_space=pl.ANY)]
    tokens = sum(left.shape[0] for left in lefts)
    return pl.pallas_call(
        weight_kernel,
        grid_spec=pltpu.PrefetchScalarGridSpec(
            num_scalar_prefetch=1,
            grid=(count,),
            in_specs=specs,
            out_specs=[
                pl.BlockSpec((CH, width), lambda j, o: (j, 0)),
                pl.BlockSpec((CH, 128), lambda j, o: (o[j], 0)),
            ],
            scratch_shapes=[pltpu.VMEM((CH, width), F32)],
        ),
        out_shape=[
            jax.ShapeDtypeStruct((count * CH, width), BF16),
            jax.ShapeDtypeStruct(sums.shape, F32),
        ],
        input_output_aliases={2 * n + 2: 1},
        cost_estimate=pl.CostEstimate(
            flops=2 * tokens * CH * count * width,
            bytes_accessed=2 * count * CH * (tokens + 2 * width),
            transcendentals=0,
        ),
        name="weight_terms",
    )(order, *lefts, *rights, w_in, sums)


def on_device(inputs, gain, w_in, grad_act, residual_gradient):
    dp_index = lax.axis_index("dp")
    t_index = lax.axis_index("tensor")
    x_at, yh_at, c_at = dp_index // 4, (dp_index // 2) % 2, dp_index % 2
    y_at, z_at = t_index // NZ, t_index % NZ

    with jax.named_scope("norm"):
        values = inputs.astype(F32)
        centered_input = values - jnp.mean(values, axis=1, keepdims=True)
        inverse_deviation = lax.rsqrt(
            jnp.mean(centered_input * centered_input, axis=1, keepdims=True) + 1e-06
        )
        standardized_input = centered_input * inverse_deviation
        normed_output = (standardized_input * gain).astype(BF16)

    with jax.named_scope("gather"):
        got = gather_tokens(normed_output)

    def act_rows(keys):
        rows = []
        for column, offset in keys:
            y = y_at if column == "A" else 1 - y_at
            start = (y * NZ + (z_at + offset) % NZ) * ROWS
            rows.append(lax.dynamic_slice_in_dim(grad_act, start, ROWS, 0))
        return jnp.concatenate(rows, 0)

    batches = (GROUPS[0] + GROUPS[1], GROUPS[2] + GROUPS[3], GROUPS[4])
    lefts, rights = [], []
    with jax.named_scope("forward"):
        for keys in batches:
            tokens = jnp.concatenate([got[key] for key in keys], 0)
            pre = jnp.dot(tokens, w_in, preferred_element_type=F32)
            unused, pullback = jax.vjp(jax.nn.gelu, pre)
            dpre = pullback(act_rows(keys).astype(F32))[0].astype(BF16)
            lefts.append(tokens)
            rights.append(lax.optimization_barrier(dpre))

    with jax.named_scope("token_gradient"):
        part = {}
        for keys, dpre in list(zip(batches, rights))[::-1]:
            product = lax.dot_general(
                dpre, w_in, (((1,), (1,)), ((), ())), preferred_element_type=F32
            ).astype(BF16)
            for at, key in enumerate(keys):
                part[key] = product[at * ROWS : (at + 1) * ROWS]

    with jax.named_scope("weight_gradient"):
        steps = ((2, 1), (2, 0), (1, 1), (3, 1), (1, 0), (3, 0), (0, 1), (0, 0))
        chunk = jnp.stack([((x_at + k) % 4) * 4 + (yh_at ^ other) * 2 for k, other in steps]).astype(jnp.int32)
        sums = jnp.zeros((w_in.shape[0], 128), F32)
        theirs, sums = weight_terms(chunk + (1 - c_at), lefts, rights, w_in, sums)
        mine, sums = weight_terms(chunk + c_at, lefts, rights, w_in, sums)

        def both(lo, hi):
            return add(mine[lo * CH : hi * CH], swap_core(theirs[lo * CH : hi * CH]))

        far = both(0, 2)
        near_other = both(2, 4)
        rest = both(4, 8)
        half = CH // 2
        up_other, down_other = near_other[:CH], near_other[CH:]
        up_own, down_own = rest[:CH], rest[CH : 2 * CH]
        here_other, here_own = rest[2 * CH : 3 * CH], rest[3 * CH :]
        far_up = to_x(jnp.concatenate([far[:half], far[CH : CH + half]], 0), 1)
        far_down = to_x(jnp.concatenate([far[half:CH], far[CH + half :]], 0), -1)
        send_up = jnp.concatenate([add(up_other[:half], far_up[:half]), up_other[half:]], 0)
        send_down = jnp.concatenate([down_other[:half], add(down_other[half:], far_down[:half])], 0)
        other = add(here_other, to_x(send_up, 1), to_x(send_down, -1))
        from_y = swap_yh(other)
        send_up = jnp.concatenate([add(up_own[:half], far_up[half:]), up_own[half:]], 0)
        send_down = jnp.concatenate([down_own[:half], add(down_own[half:], far_down[half:])], 0)
        own = (
            here_own.astype(F32)
            + to_x(send_up, 1).astype(F32)
            + to_x(send_down, -1).astype(F32)
        )
        grad_w = (own + from_y.astype(F32)) / 16

    with jax.named_scope("scale_gradient"):
        total = jnp.sum(sums, axis=1).reshape(48, 128)
        total = total + swap_core(total)
        total = total + swap_y(total)
        total = total + swap_yh(total)
        for bit in (1, 2, 4):
            total = total + ppermute(total, "tensor", lambda i: i ^ bit)
        for bit in (4, 8):
            total = total + ppermute(total, "dp", lambda i: i ^ bit)
        scale_gradient = total.reshape(-1) / gain / 16

    with jax.named_scope("scatter"):
        normed_gradient = scatter_tokens(part)

    with jax.named_scope("input_gradient"):
        scaled_gradient = normed_gradient * gain
        first_average = jnp.mean(scaled_gradient, axis=1, keepdims=True)
        second_average = jnp.mean(scaled_gradient * standardized_input, axis=1, keepdims=True)
        block_input_gradient = (
            residual_gradient.astype(F32)
            + inverse_deviation
            * (scaled_gradient - first_average - standardized_input * second_average)
        ).astype(BF16)
    return (block_input_gradient, grad_w, scale_gradient)


def solution(mesh):
    return jax.shard_map(
        on_device,
        mesh=mesh,
        in_specs=(
            P(("dp", "tensor"), None),
            P(),
            P(None, "tensor"),
            P("dp", "tensor"),
            P(("dp", "tensor"), None),
        ),
        out_specs=(P(("dp", "tensor"), None), P("dp", "tensor"), P()),
        check_vma=False,
    )
```

```python
import jax
import jax.numpy as jnp
from jax import lax
from jax.experimental import pallas as pl
from jax.experimental.pallas import tpu as pltpu
from jax.sharding import PartitionSpec as P

F32 = jnp.float32
BF16 = jnp.bfloat16
ROWS = 32
NZ = 8
CH = 384


def ppermute(value, axis, target):
    return lax.ppermute(value, axis, [(i, target(i)) for i in range(16)])


def z_shift(step):
    return lambda i: (i // NZ) * NZ + (i + step) % NZ


def to_z(value, step):
    return ppermute(value, "tensor", z_shift(step))


def swap_y(value):
    return ppermute(value, "tensor", lambda i: i ^ 8)


def to_x(value, step):
    return ppermute(value, "dp", lambda i: (i + 4 * step) % 16)


def swap_yh(value):
    return ppermute(value, "dp", lambda i: i ^ 2)


def swap_core(value):
    return ppermute(value, "dp", lambda i: i ^ 1)


def add(*terms):
    total = terms[0].astype(F32)
    for term in terms[1:]:
        total = total + term.astype(F32)
    return total.astype(BF16)


GROUPS = (
    (("A", 0), ("A", 1), ("A", -1), ("B", 0)),
    (("A", 2), ("A", -2), ("B", 1)),
    (("A", 3), ("A", -3), ("B", 2)),
    (("B", 3), ("A", 4), ("B", -2)),
    (("B", 4), ("B", -3), ("B", -1)),
)


def from_up(value):
    return to_z(value, -1)


def from_down(value):
    return to_z(value, 1)


MOVES = (
    ((("A", 1), from_up, ("A", 0)), (("A", -1), from_down, ("A", 0)), (("B", 0), swap_y, ("A", 0))),
    ((("A", 2), from_up, ("A", 1)), (("A", -2), from_down, ("A", -1)), (("B", 1), swap_y, ("A", 1))),
    ((("B", 2), swap_y, ("A", 2)), (("A", 3), from_up, ("A", 2)), (("A", -3), from_down, ("A", -2))),
    ((("B", 3), from_up, ("B", 2)), (("A", 4), from_down, ("A", -3)), (("B", -2), swap_y, ("A", -2))),
    ((("B", 4), from_up, ("B", 3)), (("B", -3), from_down, ("B", -2)), (("B", -1), swap_y, ("A", -1))),
)
def together(*values):
    return lax.optimization_barrier(values)


SMALL = pl.CostEstimate(flops=1, bytes_accessed=1, transcendentals=0)


def gelu_slope(value):
    scale = 0.7978845608028654
    square = value * value
    tanh = jnp.tanh(scale * (value + 0.044715 * (square * value)))
    return 0.5 * (1.0 + tanh) + 0.5 * value * (1.0 - tanh * tanh) * scale * (1.0 + 0.134145 * square)


def forward_kernel(slots, *refs):
    n = (len(refs) - 3) // 2
    tokens, w_ref, acts = refs[:n], refs[n], refs[n + 1 : 2 * n + 1]
    out_ref, total = refs[-2:]
    step = pl.program_id(0)
    term = jnp.dot(
        jnp.concatenate([block[...] for block in tokens], 0), w_ref[...], preferred_element_type=F32
    )

    @pl.when(step == 0)
    def _():
        total[...] = term

    @pl.when(step > 0)
    def _():
        total[...] += term

    @pl.when(step == pl.num_programs(0) - 1)
    def _():
        for at, act in enumerate(acts):
            rows = pl.ds(at * ROWS, ROWS)
            out_ref[rows, :] = (act[...].astype(F32) * gelu_slope(total[rows, :])).astype(BF16)


def forward(slots, tokens, w_in, grad_act):
    n = len(tokens)
    depth, width = w_in.shape
    part = depth // 4

    def act_spec(at):
        return pl.BlockSpec((ROWS, width), lambda j, o: (o[at], 0))

    return pl.pallas_call(
        forward_kernel,
        grid_spec=pltpu.PrefetchScalarGridSpec(
            num_scalar_prefetch=1,
            grid=(4,),
            in_specs=[pl.BlockSpec((ROWS, part), lambda j, o: (0, j))] * n
            + [pl.BlockSpec((part, width), lambda j, o: (j, 0))]
            + [act_spec(at) for at in range(n)],
            out_specs=pl.BlockSpec((n * ROWS, width), lambda j, o: (0, 0)),
            scratch_shapes=[pltpu.VMEM((n * ROWS, width), F32)],
        ),
        out_shape=jax.ShapeDtypeStruct((n * ROWS, width), BF16),
        compiler_params=pltpu.CompilerParams(vmem_limit_bytes=12 * 2**20),
        cost_estimate=SMALL,
        name="forward",
    )(slots, *tokens, w_in, *([grad_act] * n))


def backward(dpre, w_in):
    return lax.dot_general(
        dpre, w_in, (((1,), (1,)), ((), ())), preferred_element_type=F32
    ).astype(BF16)


def weight_kernel(order, place, *refs):
    blocks, rights = refs[:16], refs[16:-4]
    mine, theirs, left, turned = refs[-4:]

    @pl.when(pl.program_id(0) == 0)
    def _():
        turned[...] = jnp.concatenate([right[...] for right in rights], 0).T

    for at, block in enumerate(blocks):
        left[pl.ds(at * ROWS, ROWS), :] = block[...]
    product = jnp.dot(turned[...], left[...], preferred_element_type=F32).astype(BF16)
    for c in range(2):
        piece = product[:, c * CH : (c + 1) * CH]

        @pl.when(place[1] == c)
        def _():
            mine[0] = piece

        @pl.when(place[1] != c)
        def _():
            theirs[0] = piece


def weight_terms(order, place, blocks, rights):
    width = rights[0].shape[1]
    count = 2 * order.shape[0]
    specs = [
        pl.BlockSpec((ROWS, 2 * CH), lambda j, o, p: (0, 2 * o[j // 2] + (p[0] ^ 1 ^ (j % 2))))
    ] * 16
    specs += [pl.BlockSpec((right.shape[0], width), lambda j, o, p: (0, 0)) for right in rights]
    shape = jax.ShapeDtypeStruct((count, width, CH), BF16)
    return pl.pallas_call(
        weight_kernel,
        grid_spec=pltpu.PrefetchScalarGridSpec(
            num_scalar_prefetch=2,
            grid=(count,),
            in_specs=specs,
            out_specs=[pl.BlockSpec((1, width, CH), lambda j, o, p: (j, 0, 0))] * 2,
            scratch_shapes=[pltpu.VMEM((16 * ROWS, 2 * CH), BF16), pltpu.VMEM((width, 16 * ROWS), BF16)],
        ),
        out_shape=[shape, shape],
        compiler_params=pltpu.CompilerParams(vmem_limit_bytes=60 * 2**20),
        cost_estimate=pl.CostEstimate(
            flops=8 * 16 * ROWS * 2 * CH * count * width,
            bytes_accessed=2 * count * 2 * CH * (16 * ROWS + width),
            transcendentals=0,
        ),
        name="weight_terms",
    )(order, place, *blocks, *rights)


def place_kernel(slots, *refs):
    product, board, sems = refs[0], refs[-2], refs[-1]
    copies = []
    for at in range(product.shape[0] // ROWS):
        row = pl.multiple_of(slots[at] * ROWS, ROWS)
        copies.append(
            pltpu.make_async_copy(
                product.at[pl.ds(at * ROWS, ROWS)], board.at[pl.ds(row, ROWS)], sems.at[at]
            )
        )
        copies[-1].start()
    for copy in copies:
        copy.wait()


def place_rows(slots, product, board):
    first = board is None
    return pl.pallas_call(
        place_kernel,
        in_specs=[pl.BlockSpec(memory_space=pltpu.SMEM), pl.BlockSpec(memory_space=pl.ANY)]
        + ([] if first else [pl.BlockSpec(memory_space=pltpu.HBM)]),
        out_specs=pl.BlockSpec(memory_space=pltpu.HBM),
        out_shape=jax.ShapeDtypeStruct((16 * ROWS, product.shape[1]), BF16),
        scratch_shapes=[pltpu.SemaphoreType.DMA((product.shape[0] // ROWS,))],
        input_output_aliases={} if first else {2: 0},
        compiler_params=pltpu.CompilerParams(vmem_limit_bytes=2**20),
        cost_estimate=SMALL,
        name="place_rows",
    )(slots, product, *(() if first else (board,)))


def scale_kernel(*refs):
    blocks, products, out_ref = refs[:16], refs[16:-1], refs[-1]
    total = jnp.zeros(out_ref.shape, F32)
    at = 0
    for product in products:
        for row in range(0, product.shape[0], ROWS):
            for tile in range(0, ROWS, 16):
                left = blocks[at][pl.ds(tile, 16), :].astype(F32)
                right = product[pl.ds(row + tile, 16), :].astype(F32)
                term = left * right
                total = total + term[:8] + term[8:]
            at += 1
    out_ref[...] = total


def scale_sum(blocks, products):
    width = blocks[0].shape[1]
    cols = 1024
    return pl.pallas_call(
        scale_kernel,
        grid=(width // cols,),
        in_specs=[pl.BlockSpec((v.shape[0], cols), lambda j: (0, j)) for v in (*blocks, *products)],
        out_specs=pl.BlockSpec((8, cols), lambda j: (0, j)),
        out_shape=jax.ShapeDtypeStruct((8, width), F32),
        compiler_params=pltpu.CompilerParams(vmem_limit_bytes=60 * 2**20),
        cost_estimate=SMALL,
        name="scale_sum",
    )(*blocks, *products)


def on_device(inputs, gain, w_in, grad_act, residual_gradient):
    dp_index = lax.axis_index("dp")
    t_index = lax.axis_index("tensor")
    x_at, yh_at, c_at = dp_index // 4, (dp_index // 2) % 2, dp_index % 2
    y_at, z_at = t_index // NZ, t_index % NZ

    with jax.named_scope("norm"):
        values = inputs.astype(F32)
        centered_input = values - jnp.mean(values, axis=1, keepdims=True)
        inverse_deviation = lax.rsqrt(
            jnp.mean(centered_input * centered_input, axis=1, keepdims=True) + 1e-06
        )
        standardized_input = centered_input * inverse_deviation
        normed_output = (standardized_input * gain).astype(BF16)

    def slots(keys):
        places = [
            (y_at if column == "A" else 1 - y_at) * NZ + (z_at + offset) % NZ for column, offset in keys
        ]
        return jnp.stack(places).astype(jnp.int32)

    got = {("A", 0): normed_output}
    rights, products = [], []

    def dense(at):
        rights.append(forward(slots(GROUPS[at]), [got[key] for key in GROUPS[at]], w_in, grad_act))

    with jax.named_scope("gather"):
        for at, moves in enumerate(MOVES):
            for key, move, source in moves:
                got[key] = move(got[source])
            along_z = [key for key, move, _ in moves if move is not swap_y]
            held = [got[key] for key in along_z]
            if at >= 1:
                dense(at - 1)
                held.append(rights[-1])
            if at >= 2:
                products.append(backward(rights[at - 2], w_in))
                held.append(products[-1])
            later = [source for _, move, source in MOVES[at + 1] if move is swap_y] if at < 4 else []
            held = list(together(*held, *[got[key] for key in later if key not in along_z]))
            for key in along_z:
                got[key] = held.pop(0)
            for key in later:
                if key not in along_z:
                    got[key] = held.pop()
            if at >= 1:
                rights[-1] = held.pop(0)
            if at >= 2:
                products[-1] = held.pop(0)

    with jax.named_scope("turn"):
        products.append(backward(rights[3], w_in))
        board = None
        for keys, product in zip(GROUPS, products):
            board = place_rows(slots(keys), product, board)
        (board,) = together(board)
        dense(4)
        products.append(backward(rights[4], w_in))
        board = place_rows(slots(GROUPS[4]), products[4], board)
        blocks = [got[key] for keys in GROUPS for key in keys]

    with jax.named_scope("scatter"):
        normed_gradient = lax.psum_scatter(board, "tensor", scatter_dimension=0, tiled=True).astype(F32)

    place = jnp.stack([yh_at, c_at]).astype(jnp.int32)
    order = jnp.stack([(x_at + k) % 4 for k in (2, 1, 3, 0)]).astype(jnp.int32)
    half = w_in.shape[1] // 2

    def hop(total, axis, bit):
        return total + ppermute(total, axis, lambda i: i ^ bit)

    def moving(mine, theirs, far, chunk, way):
        first = add(mine[chunk, :half], theirs[chunk, :half], *([far[0]] if way > 0 else []))
        second = add(mine[chunk, half:], theirs[chunk, half:], *([far[0]] if way < 0 else []))
        return jnp.concatenate([first, second], 0)

    with jax.named_scope("weights"):
        first, second = together(order[:1], order[1:], products[4][:1, :1])[:2]
        far_mine, far_theirs = weight_terms(first, place, blocks, rights)
        mine, theirs = weight_terms(second, place, blocks, rights)
        sums = scale_sum(blocks, products)
        total = jnp.sum(sums, axis=0).reshape(48, 128)
        far_mine, far_theirs, mine, theirs, total = together(far_mine, far_theirs, mine, theirs, total)

    with jax.named_scope("core_far"):
        (swapped,) = together(swap_core(far_theirs))
        far, theirs, total = together(add(far_mine, swapped), theirs, total)

    with jax.named_scope("x_far"):
        far_up, far_down = to_x(far[:, :half], 1), to_x(far[:, half:], -1)
        theirs = swap_core(theirs)
        total = hop(hop(hop(total, "dp", 1), "tensor", 1), "tensor", 2)
        far_up, far_down, theirs, total = together(far_up, far_down, theirs, total)

    with jax.named_scope("x_other"):
        up_other, down_other = moving(mine, theirs, far_up[:1], 0, 1), moving(mine, theirs, far_down[:1], 2, -1)
        up_other, down_other, total = together(up_other, down_other, total)
        up_moved, down_moved = to_x(up_other, 1), to_x(down_other, -1)
        up_own, down_own = moving(mine, theirs, far_up[1:], 1, 1), moving(mine, theirs, far_down[1:], 3, -1)
        total = hop(hop(hop(total, "tensor", 4), "dp", 4), "dp", 8)
        up_moved, down_moved, up_own, down_own, total = together(
            up_moved, down_moved, up_own, down_own, total
        )

    with jax.named_scope("x_own"):
        other = add(mine[4], theirs[4], up_moved, down_moved)
        up_own, down_own, other, total = together(up_own, down_own, other, total)
        from_y = swap_yh(other)
        up_moved, down_moved = to_x(up_own, 1), to_x(down_own, -1)
        own = mine[5].astype(F32) + theirs[5].astype(F32)
        for value in (up_moved, down_moved, from_y):
            own = own + value.astype(F32)
        grad_w = (own / 16).T
        total = hop(hop(total, "dp", 2), "tensor", 8)
        scale_gradient = total.reshape(-1) / gain / 16

    with jax.named_scope("input_gradient"):
        scaled_gradient = normed_gradient * gain
        first_average = jnp.mean(scaled_gradient, axis=1, keepdims=True)
        second_average = jnp.mean(scaled_gradient * standardized_input, axis=1, keepdims=True)
        block_input_gradient = (
            residual_gradient.astype(F32)
            + inverse_deviation
            * (scaled_gradient - first_average - standardized_input * second_average)
        ).astype(BF16)
    return (block_input_gradient, grad_w, scale_gradient)


def solution(mesh):
    return jax.shard_map(
        on_device,
        mesh=mesh,
        in_specs=(
            P(("dp", "tensor"), None),
            P(),
            P(None, "tensor"),
            P("dp", "tensor"),
            P(("dp", "tensor"), None),
        ),
        out_specs=(P(("dp", "tensor"), None), P("dp", "tensor"), P()),
        check_vma=False,
    )
```

```python
import jax
import jax.numpy as jnp
from jax import lax
from jax.experimental import pallas as pl
from jax.experimental.pallas import tpu as pltpu
from jax.sharding import PartitionSpec as P

F32 = jnp.float32
BF16 = jnp.bfloat16
ROWS = 32
NZ = 8
CH = 384


def ppermute(value, axis, target):
    return lax.ppermute(value, axis, [(i, target(i)) for i in range(16)])


def z_shift(step):
    return lambda i: (i // NZ) * NZ + (i + step) % NZ


def to_z(value, step):
    return ppermute(value, "tensor", z_shift(step))


def swap_y(value):
    return ppermute(value, "tensor", lambda i: i ^ 8)


def to_x(value, step):
    return ppermute(value, "dp", lambda i: (i + 4 * step) % 16)


def swap_yh(value):
    return ppermute(value, "dp", lambda i: i ^ 2)


def swap_core(value):
    return ppermute(value, "dp", lambda i: i ^ 1)


def add(*terms):
    total = terms[0].astype(F32)
    for term in terms[1:]:
        total = total + term.astype(F32)
    return total.astype(BF16)


GROUPS = (
    (("A", 0), ("A", 1), ("A", -1), ("B", 0)),
    (("A", 2), ("A", -2), ("B", 1)),
    (("A", 3), ("A", -3), ("B", 2)),
    (("B", 3), ("A", 4), ("B", -2)),
    (("B", 4), ("B", -3), ("B", -1)),
)


def from_up(value):
    return to_z(value, -1)


def from_down(value):
    return to_z(value, 1)


MOVES = (
    ((("A", 1), from_up, ("A", 0)), (("A", -1), from_down, ("A", 0)), (("B", 0), swap_y, ("A", 0))),
    ((("A", 2), from_up, ("A", 1)), (("A", -2), from_down, ("A", -1)), (("B", 1), swap_y, ("A", 1))),
    ((("B", 2), swap_y, ("A", 2)), (("A", 3), from_up, ("A", 2)), (("A", -3), from_down, ("A", -2))),
    ((("B", 3), from_up, ("B", 2)), (("A", 4), from_down, ("A", -3)), (("B", -2), swap_y, ("A", -2))),
    ((("B", 4), from_up, ("B", 3)), (("B", -3), from_down, ("B", -2)), (("B", -1), swap_y, ("A", -1))),
)
def together(*values):
    return lax.optimization_barrier(values)


SMALL = pl.CostEstimate(flops=1, bytes_accessed=1, transcendentals=0)


def gelu_slope(value):
    scale = 0.7978845608028654
    square = value * value
    tanh = jnp.tanh(scale * (value + 0.044715 * (square * value)))
    return 0.5 * (1.0 + tanh) + 0.5 * value * (1.0 - tanh * tanh) * scale * (1.0 + 0.134145 * square)


def forward_kernel(slots, *refs):
    n = (len(refs) - 3) // 2
    tokens, w_ref, acts = refs[:n], refs[n], refs[n + 1 : 2 * n + 1]
    out_ref, total = refs[-2:]
    step = pl.program_id(0)
    term = jnp.dot(
        jnp.concatenate([block[...] for block in tokens], 0), w_ref[...], preferred_element_type=F32
    )

    @pl.when(step == 0)
    def _():
        total[...] = term

    @pl.when(step > 0)
    def _():
        total[...] += term

    @pl.when(step == pl.num_programs(0) - 1)
    def _():
        for at, act in enumerate(acts):
            rows = pl.ds(at * ROWS, ROWS)
            out_ref[rows, :] = (act[...].astype(F32) * gelu_slope(total[rows, :])).astype(BF16)


def forward(slots, tokens, w_in, grad_act):
    n = len(tokens)
    depth, width = w_in.shape
    part = depth // 4

    def act_spec(at):
        return pl.BlockSpec((ROWS, width), lambda j, o: (o[at], 0))

    return pl.pallas_call(
        forward_kernel,
        grid_spec=pltpu.PrefetchScalarGridSpec(
            num_scalar_prefetch=1,
            grid=(4,),
            in_specs=[pl.BlockSpec((ROWS, part), lambda j, o: (0, j))] * n
            + [pl.BlockSpec((part, width), lambda j, o: (j, 0))]
            + [act_spec(at) for at in range(n)],
            out_specs=pl.BlockSpec((n * ROWS, width), lambda j, o: (0, 0)),
            scratch_shapes=[pltpu.VMEM((n * ROWS, width), F32)],
        ),
        out_shape=jax.ShapeDtypeStruct((n * ROWS, width), BF16),
        compiler_params=pltpu.CompilerParams(vmem_limit_bytes=12 * 2**20),
        cost_estimate=SMALL,
        name="forward",
    )(slots, *tokens, w_in, *([grad_act] * n))


def backward(dpre, w_in):
    return lax.dot_general(
        dpre, w_in, (((1,), (1,)), ((), ())), preferred_element_type=F32
    ).astype(BF16)


def weight_kernel(order, place, *refs):
    blocks, rights = refs[:16], refs[16:-4]
    mine, theirs, left, turned = refs[-4:]

    @pl.when(pl.program_id(0) == 0)
    def _():
        turned[...] = jnp.concatenate([right[...] for right in rights], 0).T

    for at, block in enumerate(blocks):
        left[pl.ds(at * ROWS, ROWS), :] = block[...]
    product = jnp.dot(turned[...], left[...], preferred_element_type=F32).astype(BF16)
    for c in range(2):
        piece = product[:, c * CH : (c + 1) * CH]

        @pl.when(place[1] == c)
        def _():
            mine[0] = piece

        @pl.when(place[1] != c)
        def _():
            theirs[0] = piece


def weight_terms(order, place, blocks, rights):
    width = rights[0].shape[1]
    count = 2 * order.shape[0]
    specs = [
        pl.BlockSpec((ROWS, 2 * CH), lambda j, o, p: (0, 2 * o[j // 2] + (p[0] ^ 1 ^ (j % 2))))
    ] * 16
    specs += [pl.BlockSpec((right.shape[0], width), lambda j, o, p: (0, 0)) for right in rights]
    shape = jax.ShapeDtypeStruct((count, width, CH), BF16)
    return pl.pallas_call(
        weight_kernel,
        grid_spec=pltpu.PrefetchScalarGridSpec(
            num_scalar_prefetch=2,
            grid=(count,),
            in_specs=specs,
            out_specs=[pl.BlockSpec((1, width, CH), lambda j, o, p: (j, 0, 0))] * 2,
            scratch_shapes=[pltpu.VMEM((16 * ROWS, 2 * CH), BF16), pltpu.VMEM((width, 16 * ROWS), BF16)],
        ),
        out_shape=[shape, shape],
        compiler_params=pltpu.CompilerParams(vmem_limit_bytes=60 * 2**20),
        cost_estimate=pl.CostEstimate(
            flops=8 * 16 * ROWS * 2 * CH * count * width,
            bytes_accessed=2 * count * 2 * CH * (16 * ROWS + width),
            transcendentals=0,
        ),
        name="weight_terms",
    )(order, place, *blocks, *rights)


def place_kernel(slots, *refs):
    sources, board, sems = refs[:-2], refs[-2], refs[-1]
    copies = []
    for source in sources:
        for row in range(0, source.shape[0], ROWS):
            at = len(copies)
            into = pl.multiple_of(slots[at] * ROWS, ROWS)
            copies.append(
                pltpu.make_async_copy(
                    source.at[pl.ds(row, ROWS)], board.at[pl.ds(into, ROWS)], sems.at[at]
                )
            )
            copies[-1].start()
    for copy in copies:
        copy.wait()


def place_rows(slots, sources):
    return pl.pallas_call(
        place_kernel,
        in_specs=[pl.BlockSpec(memory_space=pltpu.SMEM)]
        + [pl.BlockSpec(memory_space=pl.ANY)] * len(sources),
        out_specs=pl.BlockSpec(memory_space=pl.ANY),
        out_shape=jax.ShapeDtypeStruct((16 * ROWS, sources[0].shape[1]), BF16),
        scratch_shapes=[pltpu.SemaphoreType.DMA((16,))],
        compiler_params=pltpu.CompilerParams(vmem_limit_bytes=2**20),
        cost_estimate=SMALL,
        name="place_rows",
    )(slots, *sources)


def scale_kernel(slots, *refs):
    blocks, product, out_ref = refs[:16], refs[16], refs[17]
    total = jnp.zeros(out_ref.shape, F32)
    for at, block in enumerate(blocks):
        row = pl.multiple_of(slots[at] * ROWS, ROWS)
        for tile in range(0, ROWS, 16):
            left = block[pl.ds(tile, 16), :].astype(F32)
            right = product[pl.ds(row + tile, 16), :].astype(F32)
            term = left * right
            total = total + term[:8] + term[8:]
    out_ref[...] = total


def scale_sum(slots, blocks, product):
    width = product.shape[1]
    cols = 1024
    return pl.pallas_call(
        scale_kernel,
        grid_spec=pltpu.PrefetchScalarGridSpec(
            num_scalar_prefetch=1,
            grid=(width // cols,),
            in_specs=[pl.BlockSpec((v.shape[0], cols), lambda j, o: (0, j)) for v in (*blocks, product)],
            out_specs=pl.BlockSpec((8, cols), lambda j, o: (0, j)),
        ),
        out_shape=jax.ShapeDtypeStruct((8, width), F32),
        compiler_params=pltpu.CompilerParams(vmem_limit_bytes=60 * 2**20),
        cost_estimate=SMALL,
        name="scale_sum",
    )(slots, *blocks, product)


def on_device(inputs, gain, w_in, grad_act, residual_gradient):
    dp_index = lax.axis_index("dp")
    t_index = lax.axis_index("tensor")
    x_at, yh_at, c_at = dp_index // 4, (dp_index // 2) % 2, dp_index % 2
    y_at, z_at = t_index // NZ, t_index % NZ

    with jax.named_scope("norm"):
        values = inputs.astype(F32)
        centered_input = values - jnp.mean(values, axis=1, keepdims=True)
        inverse_deviation = lax.rsqrt(
            jnp.mean(centered_input * centered_input, axis=1, keepdims=True) + 1e-06
        )
        standardized_input = centered_input * inverse_deviation
        normed_output = (standardized_input * gain).astype(BF16)

    def slots(keys):
        places = [
            (y_at if column == "A" else 1 - y_at) * NZ + (z_at + offset) % NZ for column, offset in keys
        ]
        return jnp.stack(places).astype(jnp.int32)

    got = {("A", 0): normed_output}
    rights = []

    def dense(at):
        rights.append(forward(slots(GROUPS[at]), [got[key] for key in GROUPS[at]], w_in, grad_act))

    with jax.named_scope("gather"):
        for at, moves in enumerate(MOVES):
            for key, move, source in moves:
                got[key] = move(got[source])
            along_z = [key for key, move, _ in moves if move is not swap_y]
            held = [got[key] for key in along_z]
            if at >= 1:
                dense(at - 1)
                held.append(rights[-1])
            later = [source for _, move, source in MOVES[at + 1] if move is swap_y] if at < 4 else []
            held = list(together(*held, *[got[key] for key in later if key not in along_z]))
            for key in along_z:
                got[key] = held.pop(0)
            for key in later:
                if key not in along_z:
                    got[key] = held.pop()
            if at >= 1:
                rights[-1] = held.pop(0)

    with jax.named_scope("turn"):
        dense(4)
        blocks = [got[key] for keys in GROUPS for key in keys]
        rows = slots([key for keys in GROUPS for key in keys])
        product = backward(place_rows(rows, rights), w_in)

    with jax.named_scope("scatter"):
        normed_gradient = lax.psum_scatter(product, "tensor", scatter_dimension=0, tiled=True).astype(F32)

    place = jnp.stack([yh_at, c_at]).astype(jnp.int32)
    order = jnp.stack([(x_at + k) % 4 for k in (2, 1, 3, 0)]).astype(jnp.int32)
    half = w_in.shape[1] // 2

    def hop(total, axis, bit):
        return total + ppermute(total, axis, lambda i: i ^ bit)

    def moving(mine, theirs, far, chunk, way):
        first = add(mine[chunk, :half], theirs[chunk, :half], *([far[0]] if way > 0 else []))
        second = add(mine[chunk, half:], theirs[chunk, half:], *([far[0]] if way < 0 else []))
        return jnp.concatenate([first, second], 0)

    with jax.named_scope("weights"):
        first, second = together(order[:1], order[1:], product[:1, :1])[:2]
        far_mine, far_theirs = weight_terms(first, place, blocks, rights)
        sums = scale_sum(rows, blocks, product)
        total = jnp.sum(sums, axis=0).reshape(48, 128)
        far_mine, far_theirs, second, total = together(far_mine, far_theirs, second, total)
        mine, theirs = weight_terms(second, place, blocks, rights)
        total = hop(hop(total, "dp", 1), "tensor", 1)
        far_mine, far_theirs, mine, theirs, total = together(far_mine, far_theirs, mine, theirs, total)

    with jax.named_scope("core_far"):
        (swapped,) = together(swap_core(far_theirs))
        far, theirs, total = together(add(far_mine, swapped), theirs, total)

    with jax.named_scope("x_far"):
        far_up, far_down = to_x(far[:, :half], 1), to_x(far[:, half:], -1)
        theirs = swap_core(theirs)
        total = hop(hop(hop(total, "tensor", 2), "tensor", 4), "dp", 4)
        far_up, far_down, theirs, total = together(far_up, far_down, theirs, total)

    with jax.named_scope("x_other"):
        up_other, down_other = moving(mine, theirs, far_up[:1], 0, 1), moving(mine, theirs, far_down[:1], 2, -1)
        up_other, down_other, total = together(up_other, down_other, total)
        up_moved, down_moved = to_x(up_other, 1), to_x(down_other, -1)
        up_own, down_own = moving(mine, theirs, far_up[1:], 1, 1), moving(mine, theirs, far_down[1:], 3, -1)
        total = hop(hop(total, "dp", 8), "dp", 2)
        up_moved, down_moved, up_own, down_own, total = together(
            up_moved, down_moved, up_own, down_own, total
        )

    with jax.named_scope("x_own"):
        other = add(mine[4], theirs[4], up_moved, down_moved)
        up_own, down_own, other, total = together(up_own, down_own, other, total)
        from_y = swap_yh(other)
        up_moved, down_moved = to_x(up_own, 1), to_x(down_own, -1)
        own = mine[5].astype(F32) + theirs[5].astype(F32)
        for value in (up_moved, down_moved, from_y):
            own = own + value.astype(F32)
        grad_w = (own / 16).T
        total = hop(total, "tensor", 8)
        scale_gradient = total.reshape(-1) / gain / 16

    with jax.named_scope("input_gradient"):
        scaled_gradient = normed_gradient * gain
        first_average = jnp.mean(scaled_gradient, axis=1, keepdims=True)
        second_average = jnp.mean(scaled_gradient * standardized_input, axis=1, keepdims=True)
        block_input_gradient = (
            residual_gradient.astype(F32)
            + inverse_deviation
            * (scaled_gradient - first_average - standardized_input * second_average)
        ).astype(BF16)
    return (block_input_gradient, grad_w, scale_gradient)


def solution(mesh):
    return jax.shard_map(
        on_device,
        mesh=mesh,
        in_specs=(
            P(("dp", "tensor"), None),
            P(),
            P(None, "tensor"),
            P("dp", "tensor"),
            P(("dp", "tensor"), None),
        ),
        out_specs=(P(("dp", "tensor"), None), P("dp", "tensor"), P()),
        check_vma=False,
    )
```

```python
import jax
import jax.numpy as jnp
from jax import lax
from jax.experimental import pallas as pl
from jax.experimental.pallas import tpu as pltpu
from jax.sharding import PartitionSpec as P

F32 = jnp.float32
BF16 = jnp.bfloat16
ROWS = 32
NZ = 8
CH = 384


def ppermute(value, axis, target):
    return lax.ppermute(value, axis, [(i, target(i)) for i in range(16)])


def z_shift(step):
    return lambda i: (i // NZ) * NZ + (i + step) % NZ


def to_z(value, step):
    return ppermute(value, "tensor", z_shift(step))


def swap_y(value):
    return ppermute(value, "tensor", lambda i: i ^ 8)


def to_x(value, step):
    return ppermute(value, "dp", lambda i: (i + 4 * step) % 16)


def swap_yh(value):
    return ppermute(value, "dp", lambda i: i ^ 2)


def swap_core(value):
    return ppermute(value, "dp", lambda i: i ^ 1)


def add(*terms):
    total = terms[0].astype(F32)
    for term in terms[1:]:
        total = total + term.astype(F32)
    return total.astype(BF16)


GROUPS = (
    (("A", 0), ("A", 1), ("A", -1), ("B", 0)),
    (("A", 2), ("A", -2), ("B", 1)),
    (("A", 3), ("A", -3), ("B", 2)),
    (("B", 3), ("A", 4), ("B", -2)),
    (("B", 4), ("B", -3), ("B", -1)),
)


def from_up(value):
    return to_z(value, -1)


def from_down(value):
    return to_z(value, 1)


MOVES = (
    ((("A", 1), from_up, ("A", 0)), (("A", -1), from_down, ("A", 0)), (("B", 0), swap_y, ("A", 0))),
    ((("A", 2), from_up, ("A", 1)), (("A", -2), from_down, ("A", -1)), (("B", 1), swap_y, ("A", 1))),
    ((("B", 2), swap_y, ("A", 2)), (("A", 3), from_up, ("A", 2)), (("A", -3), from_down, ("A", -2))),
    ((("B", 3), from_up, ("B", 2)), (("A", 4), from_down, ("A", -3)), (("B", -2), swap_y, ("A", -2))),
    ((("B", 4), from_up, ("B", 3)), (("B", -3), from_down, ("B", -2)), (("B", -1), swap_y, ("A", -1))),
)
def together(*values):
    return lax.optimization_barrier(values)


SMALL = pl.CostEstimate(flops=1, bytes_accessed=1, transcendentals=0)


def gelu_slope(value):
    scale = 0.7978845608028654
    square = value * value
    tanh = jnp.tanh(scale * (value + 0.044715 * (square * value)))
    return 0.5 * (1.0 + tanh) + 0.5 * value * (1.0 - tanh * tanh) * scale * (1.0 + 0.134145 * square)


def forward_kernel(slots, *refs):
    n = (len(refs) - 3) // 2
    tokens, w_ref, acts = refs[:n], refs[n], refs[n + 1 : 2 * n + 1]
    out_ref, total = refs[-2:]
    step = pl.program_id(0)
    term = jnp.dot(
        jnp.concatenate([block[...] for block in tokens], 0), w_ref[...], preferred_element_type=F32
    )

    @pl.when(step == 0)
    def _():
        total[...] = term

    @pl.when(step > 0)
    def _():
        total[...] += term

    @pl.when(step == pl.num_programs(0) - 1)
    def _():
        for at, act in enumerate(acts):
            rows = pl.ds(at * ROWS, ROWS)
            out_ref[rows, :] = (act[...].astype(F32) * gelu_slope(total[rows, :])).astype(BF16)


def forward(slots, tokens, w_in, grad_act):
    n = len(tokens)
    depth, width = w_in.shape
    part = depth // 4

    def act_spec(at):
        return pl.BlockSpec((ROWS, width), lambda j, o: (o[at], 0))

    return pl.pallas_call(
        forward_kernel,
        grid_spec=pltpu.PrefetchScalarGridSpec(
            num_scalar_prefetch=1,
            grid=(4,),
            in_specs=[pl.BlockSpec((ROWS, part), lambda j, o: (0, j))] * n
            + [pl.BlockSpec((part, width), lambda j, o: (j, 0))]
            + [act_spec(at) for at in range(n)],
            out_specs=pl.BlockSpec((n * ROWS, width), lambda j, o: (0, 0)),
            scratch_shapes=[pltpu.VMEM((n * ROWS, width), F32)],
        ),
        out_shape=jax.ShapeDtypeStruct((n * ROWS, width), BF16),
        compiler_params=pltpu.CompilerParams(vmem_limit_bytes=12 * 2**20),
        cost_estimate=SMALL,
        name="forward",
    )(slots, *tokens, w_in, *([grad_act] * n))


def backward(dpre, w_in):
    return lax.dot_general(
        dpre, w_in, (((1,), (1,)), ((), ())), preferred_element_type=F32
    ).astype(BF16)


def weight_kernel(order, place, *refs):
    blocks, rights = refs[:16], refs[16:-4]
    mine, theirs, left, turned = refs[-4:]

    @pl.when(pl.program_id(0) == 0)
    def _():
        turned[...] = jnp.concatenate([right[...] for right in rights], 0).T

    for at, block in enumerate(blocks):
        left[pl.ds(at * ROWS, ROWS), :] = block[...]
    product = jnp.dot(turned[...], left[...], preferred_element_type=F32).astype(BF16)
    for c in range(2):
        piece = product[:, c * CH : (c + 1) * CH]

        @pl.when(place[1] == c)
        def _():
            mine[0] = piece

        @pl.when(place[1] != c)
        def _():
            theirs[0] = piece


def weight_terms(order, place, blocks, rights):
    width = rights[0].shape[1]
    count = 2 * order.shape[0]
    specs = [
        pl.BlockSpec((ROWS, 2 * CH), lambda j, o, p: (0, 2 * o[j // 2] + (p[0] ^ 1 ^ (j % 2))))
    ] * 16
    specs += [pl.BlockSpec((right.shape[0], width), lambda j, o, p: (0, 0)) for right in rights]
    shape = jax.ShapeDtypeStruct((count, width, CH), BF16)
    return pl.pallas_call(
        weight_kernel,
        grid_spec=pltpu.PrefetchScalarGridSpec(
            num_scalar_prefetch=2,
            grid=(count,),
            in_specs=specs,
            out_specs=[pl.BlockSpec((1, width, CH), lambda j, o, p: (j, 0, 0))] * 2,
            scratch_shapes=[pltpu.VMEM((16 * ROWS, 2 * CH), BF16), pltpu.VMEM((width, 16 * ROWS), BF16)],
        ),
        out_shape=[shape, shape],
        compiler_params=pltpu.CompilerParams(vmem_limit_bytes=60 * 2**20),
        cost_estimate=pl.CostEstimate(
            flops=8 * 16 * ROWS * 2 * CH * count * width,
            bytes_accessed=2 * count * 2 * CH * (16 * ROWS + width),
            transcendentals=0,
        ),
        name="weight_terms",
    )(order, place, *blocks, *rights)


def place_kernel(slots, *refs):
    sources, board, sems = refs[:-2], refs[-2], refs[-1]
    copies = []
    for source in sources:
        for row in range(0, source.shape[0], ROWS):
            at = len(copies)
            into = pl.multiple_of(slots[at] * ROWS, ROWS)
            copies.append(
                pltpu.make_async_copy(
                    source.at[pl.ds(row, ROWS)], board.at[pl.ds(into, ROWS)], sems.at[at]
                )
            )
            copies[-1].start()
    for copy in copies:
        copy.wait()


def place_rows(slots, sources):
    return pl.pallas_call(
        place_kernel,
        in_specs=[pl.BlockSpec(memory_space=pltpu.SMEM)]
        + [pl.BlockSpec(memory_space=pl.ANY)] * len(sources),
        out_specs=pl.BlockSpec(memory_space=pl.ANY),
        out_shape=jax.ShapeDtypeStruct((16 * ROWS, sources[0].shape[1]), BF16),
        scratch_shapes=[pltpu.SemaphoreType.DMA((16,))],
        compiler_params=pltpu.CompilerParams(vmem_limit_bytes=2**20),
        cost_estimate=SMALL,
        name="place_rows",
    )(slots, *sources)


def scale_kernel(slots, *refs):
    blocks, product, out_ref = refs[:16], refs[16], refs[17]
    total = jnp.zeros(out_ref.shape, F32)
    for at, block in enumerate(blocks):
        row = pl.multiple_of(slots[at] * ROWS, ROWS)
        for tile in range(0, ROWS, 16):
            left = block[pl.ds(tile, 16), :].astype(F32)
            right = product[pl.ds(row + tile, 16), :].astype(F32)
            term = left * right
            total = total + term[:8] + term[8:]
    out_ref[...] = total


def scale_sum(slots, blocks, product):
    width = product.shape[1]
    cols = 1024
    return pl.pallas_call(
        scale_kernel,
        grid_spec=pltpu.PrefetchScalarGridSpec(
            num_scalar_prefetch=1,
            grid=(width // cols,),
            in_specs=[pl.BlockSpec((v.shape[0], cols), lambda j, o: (0, j)) for v in (*blocks, product)],
            out_specs=pl.BlockSpec((8, cols), lambda j, o: (0, j)),
        ),
        out_shape=jax.ShapeDtypeStruct((8, width), F32),
        compiler_params=pltpu.CompilerParams(vmem_limit_bytes=60 * 2**20),
        cost_estimate=SMALL,
        name="scale_sum",
    )(slots, *blocks, product)


def on_device(inputs, gain, w_in, grad_act, residual_gradient):
    dp_index = lax.axis_index("dp")
    t_index = lax.axis_index("tensor")
    x_at, yh_at, c_at = dp_index // 4, (dp_index // 2) % 2, dp_index % 2
    y_at, z_at = t_index // NZ, t_index % NZ

    with jax.named_scope("norm"):
        values = inputs.astype(F32)
        centered_input = values - jnp.mean(values, axis=1, keepdims=True)
        inverse_deviation = lax.rsqrt(
            jnp.mean(centered_input * centered_input, axis=1, keepdims=True) + 1e-06
        )
        standardized_input = centered_input * inverse_deviation
        normed_output = (standardized_input * gain).astype(BF16)

    def slots(keys):
        places = [
            (y_at if column == "A" else 1 - y_at) * NZ + (z_at + offset) % NZ for column, offset in keys
        ]
        return jnp.stack(places).astype(jnp.int32)

    place = jnp.stack([yh_at, c_at]).astype(jnp.int32)
    order = jnp.stack([(x_at + k) % 4 for k in (2, 1, 3, 0)]).astype(jnp.int32)
    got = {("A", 0): normed_output}
    rights = []

    def dense(at):
        rights.append(forward(slots(GROUPS[at]), [got[key] for key in GROUPS[at]], w_in, grad_act))

    with jax.named_scope("gather"):
        for at, moves in enumerate(MOVES):
            for key, move, source in moves:
                got[key] = move(got[source])
            if at == 2:
                got["A", 3], order, place = together(got["A", 3], order, place)
            along_z = [key for key, move, _ in moves if move is not swap_y]
            held = [got[key] for key in along_z]
            if at >= 1:
                dense(at - 1)
                held.append(rights[-1])
            later = [source for _, move, source in MOVES[at + 1] if move is swap_y] if at < 4 else []
            held = list(together(*held, *[got[key] for key in later if key not in along_z]))
            for key in along_z:
                got[key] = held.pop(0)
            for key in later:
                if key not in along_z:
                    got[key] = held.pop()
            if at >= 1:
                rights[-1] = held.pop(0)

    with jax.named_scope("turn"):
        dense(4)
        blocks = [got[key] for keys in GROUPS for key in keys]
        rows = slots([key for keys in GROUPS for key in keys])
        product = backward(place_rows(rows, rights), w_in)

    with jax.named_scope("scatter"):
        normed_gradient = lax.psum_scatter(product, "tensor", scatter_dimension=0, tiled=True).astype(F32)

    half = w_in.shape[1] // 2

    def hop(total, axis, bit):
        return total + ppermute(total, axis, lambda i: i ^ bit)

    def moving(mine, theirs, far, chunk, way):
        first = add(mine[chunk, :half], theirs[chunk, :half], *([far[0]] if way > 0 else []))
        second = add(mine[chunk, half:], theirs[chunk, half:], *([far[0]] if way < 0 else []))
        return jnp.concatenate([first, second], 0)

    with jax.named_scope("weights"):
        first, second = together(order[:1], order[1:], product[:1, :1])[:2]
        far_mine, far_theirs = weight_terms(first, place, blocks, rights)
        sums = scale_sum(rows, blocks, product)
        total = jnp.sum(sums, axis=0).reshape(48, 128)
        far_mine, far_theirs, second, total = together(far_mine, far_theirs, second, total)
        mine, theirs = weight_terms(second, place, blocks, rights)
        total = hop(hop(total, "dp", 1), "dp", 4)
        far_mine, far_theirs, mine, theirs, total = together(far_mine, far_theirs, mine, theirs, total)

    with jax.named_scope("core_far"):
        (swapped,) = together(swap_core(far_theirs))
        far, theirs, total = together(add(far_mine, swapped), theirs, total)

    with jax.named_scope("x_far"):
        far_up, far_down = to_x(far[:, :half], 1), to_x(far[:, half:], -1)
        theirs = swap_core(theirs)
        total = hop(total, "dp", 2)
        far_up, far_down, theirs, total = together(far_up, far_down, theirs, total)

    with jax.named_scope("x_other"):
        up_other, down_other = moving(mine, theirs, far_up[:1], 0, 1), moving(mine, theirs, far_down[:1], 2, -1)
        up_other, down_other, total = together(up_other, down_other, total)
        up_moved, down_moved = to_x(up_other, 1), to_x(down_other, -1)
        up_own, down_own = moving(mine, theirs, far_up[1:], 1, 1), moving(mine, theirs, far_down[1:], 3, -1)
        total = hop(hop(hop(total, "tensor", 1), "tensor", 2), "tensor", 4)
        up_moved, down_moved, up_own, down_own, total = together(
            up_moved, down_moved, up_own, down_own, total
        )

    with jax.named_scope("x_own"):
        other = add(mine[4], theirs[4], up_moved, down_moved)
        up_own, down_own, other, total = together(up_own, down_own, other, total)
        from_y = swap_yh(other)
        up_moved, down_moved = to_x(up_own, 1), to_x(down_own, -1)
        own = mine[5].astype(F32) + theirs[5].astype(F32)
        for value in (up_moved, down_moved, from_y):
            own = own + value.astype(F32)
        grad_w = (own / 16).T
        last = ppermute(total, "dp", lambda i: i ^ 8)

    with jax.named_scope("input_gradient"):
        scaled_gradient = normed_gradient * gain
        first_average = jnp.mean(scaled_gradient, axis=1, keepdims=True)
        second_average = jnp.mean(scaled_gradient * standardized_input, axis=1, keepdims=True)
        block_input_gradient = (
            residual_gradient.astype(F32)
            + inverse_deviation
            * (scaled_gradient - first_average - standardized_input * second_average)
        ).astype(BF16)
    with jax.named_scope("scale_gradient"):
        last, block_input_gradient = together(last, block_input_gradient)
        scale_gradient = hop(total + last, "tensor", 8).reshape(-1) / gain / 16
    return (block_input_gradient, grad_w, scale_gradient)


def solution(mesh):
    return jax.shard_map(
        on_device,
        mesh=mesh,
        in_specs=(
            P(("dp", "tensor"), None),
            P(),
            P(None, "tensor"),
            P("dp", "tensor"),
            P(("dp", "tensor"), None),
        ),
        out_specs=(P(("dp", "tensor"), None), P("dp", "tensor"), P()),
        check_vma=False,
    )
```

```python
import jax
import jax.numpy as jnp
from jax import lax
from jax.experimental import pallas as pl
from jax.experimental.pallas import tpu as pltpu
from jax.sharding import PartitionSpec as P

F32 = jnp.float32
BF16 = jnp.bfloat16
ROWS = 32
NZ = 8
CH = 384


def ppermute(value, axis, target):
    return lax.ppermute(value, axis, [(i, target(i)) for i in range(16)])


def z_shift(step):
    return lambda i: (i // NZ) * NZ + (i + step) % NZ


def to_z(value, step):
    return ppermute(value, "tensor", z_shift(step))


def swap_y(value):
    return ppermute(value, "tensor", lambda i: i ^ 8)


def to_x(value, step):
    return ppermute(value, "dp", lambda i: (i + 4 * step) % 16)


def swap_yh(value):
    return ppermute(value, "dp", lambda i: i ^ 2)


def swap_core(value):
    return ppermute(value, "dp", lambda i: i ^ 1)


def add(*terms):
    total = terms[0].astype(F32)
    for term in terms[1:]:
        total = total + term.astype(F32)
    return total.astype(BF16)


GROUPS = (
    (("A", 0), ("A", 1), ("A", -1), ("B", 0)),
    (("A", 2), ("A", -2), ("B", 1)),
    (("A", 3), ("A", -3), ("B", 2)),
    (("B", 3), ("A", 4), ("B", -2)),
    (("B", 4), ("B", -3), ("B", -1)),
)


def from_up(value):
    return to_z(value, -1)


def from_down(value):
    return to_z(value, 1)


MOVES = (
    ((("A", 1), from_up, ("A", 0)), (("A", -1), from_down, ("A", 0)), (("B", 0), swap_y, ("A", 0))),
    ((("A", 2), from_up, ("A", 1)), (("A", -2), from_down, ("A", -1)), (("B", 1), swap_y, ("A", 1))),
    ((("B", 2), swap_y, ("A", 2)), (("A", 3), from_up, ("A", 2)), (("A", -3), from_down, ("A", -2))),
    ((("B", 3), from_up, ("B", 2)), (("A", 4), from_down, ("A", -3)), (("B", -2), swap_y, ("A", -2))),
    ((("B", 4), from_up, ("B", 3)), (("B", -3), from_down, ("B", -2)), (("B", -1), swap_y, ("A", -1))),
)
def together(*values):
    return lax.optimization_barrier(values)


SMALL = pl.CostEstimate(flops=1, bytes_accessed=1, transcendentals=0)


def gelu_slope(value):
    scale = 0.7978845608028654
    square = value * value
    tanh = jnp.tanh(scale * (value + 0.044715 * (square * value)))
    return 0.5 * (1.0 + tanh) + 0.5 * value * (1.0 - tanh * tanh) * scale * (1.0 + 0.134145 * square)


def forward_kernel(slots, *refs):
    n = (len(refs) - 3) // 2
    tokens, w_ref, acts = refs[:n], refs[n], refs[n + 1 : 2 * n + 1]
    out_ref, total = refs[-2:]
    step = pl.program_id(0)
    term = jnp.dot(
        jnp.concatenate([block[...] for block in tokens], 0), w_ref[...], preferred_element_type=F32
    )

    @pl.when(step == 0)
    def _():
        total[...] = term

    @pl.when(step > 0)
    def _():
        total[...] += term

    @pl.when(step == pl.num_programs(0) - 1)
    def _():
        for at, act in enumerate(acts):
            rows = pl.ds(at * ROWS, ROWS)
            out_ref[rows, :] = (act[...].astype(F32) * gelu_slope(total[rows, :])).astype(BF16)


def forward(slots, tokens, w_in, grad_act):
    n = len(tokens)
    depth, width = w_in.shape
    part = depth // 4

    def act_spec(at):
        return pl.BlockSpec((ROWS, width), lambda j, o: (o[at], 0))

    return pl.pallas_call(
        forward_kernel,
        grid_spec=pltpu.PrefetchScalarGridSpec(
            num_scalar_prefetch=1,
            grid=(4,),
            in_specs=[pl.BlockSpec((ROWS, part), lambda j, o: (0, j))] * n
            + [pl.BlockSpec((part, width), lambda j, o: (j, 0))]
            + [act_spec(at) for at in range(n)],
            out_specs=pl.BlockSpec((n * ROWS, width), lambda j, o: (0, 0)),
            scratch_shapes=[pltpu.VMEM((n * ROWS, width), F32)],
        ),
        out_shape=jax.ShapeDtypeStruct((n * ROWS, width), BF16),
        compiler_params=pltpu.CompilerParams(vmem_limit_bytes=12 * 2**20),
        cost_estimate=SMALL,
        name="forward",
    )(slots, *tokens, w_in, *([grad_act] * n))


def backward(dpre, w_in):
    return lax.dot_general(
        dpre, w_in, (((1,), (1,)), ((), ())), preferred_element_type=F32
    ).astype(BF16)


def weight_kernel(order, place, *refs):
    blocks, rights = refs[:16], refs[16:-4]
    mine, theirs, left, turned = refs[-4:]

    @pl.when(pl.program_id(0) == 0)
    def _():
        turned[...] = jnp.concatenate([right[...] for right in rights], 0).T

    for at, block in enumerate(blocks):
        left[pl.ds(at * ROWS, ROWS), :] = block[...]
    product = jnp.dot(turned[...], left[...], preferred_element_type=F32).astype(BF16)
    for c in range(2):
        piece = product[:, c * CH : (c + 1) * CH]

        @pl.when(place[1] == c)
        def _():
            mine[0] = piece

        @pl.when(place[1] != c)
        def _():
            theirs[0] = piece


def weight_terms(order, place, blocks, rights):
    width = rights[0].shape[1]
    count = 2 * order.shape[0]
    specs = [
        pl.BlockSpec((ROWS, 2 * CH), lambda j, o, p: (0, 2 * o[j // 2] + (p[0] ^ 1 ^ (j % 2))))
    ] * 16
    specs += [pl.BlockSpec((right.shape[0], width), lambda j, o, p: (0, 0)) for right in rights]
    shape = jax.ShapeDtypeStruct((count, width, CH), BF16)
    return pl.pallas_call(
        weight_kernel,
        grid_spec=pltpu.PrefetchScalarGridSpec(
            num_scalar_prefetch=2,
            grid=(count,),
            in_specs=specs,
            out_specs=[pl.BlockSpec((1, width, CH), lambda j, o, p: (j, 0, 0))] * 2,
            scratch_shapes=[pltpu.VMEM((16 * ROWS, 2 * CH), BF16), pltpu.VMEM((width, 16 * ROWS), BF16)],
        ),
        out_shape=[shape, shape],
        compiler_params=pltpu.CompilerParams(vmem_limit_bytes=60 * 2**20),
        cost_estimate=pl.CostEstimate(
            flops=8 * 16 * ROWS * 2 * CH * count * width,
            bytes_accessed=2 * count * 2 * CH * (16 * ROWS + width),
            transcendentals=0,
        ),
        name="weight_terms",
    )(order, place, *blocks, *rights)


def place_kernel(slots, *refs):
    sources, board, sems = refs[:-2], refs[-2], refs[-1]
    copies = []
    for source in sources:
        for row in range(0, source.shape[0], ROWS):
            at = len(copies)
            into = pl.multiple_of(slots[at] * ROWS, ROWS)
            copies.append(
                pltpu.make_async_copy(
                    source.at[pl.ds(row, ROWS)], board.at[pl.ds(into, ROWS)], sems.at[at]
                )
            )
            copies[-1].start()
    for copy in copies:
        copy.wait()


def place_rows(slots, sources):
    return pl.pallas_call(
        place_kernel,
        in_specs=[pl.BlockSpec(memory_space=pltpu.SMEM)]
        + [pl.BlockSpec(memory_space=pl.ANY)] * len(sources),
        out_specs=pl.BlockSpec(memory_space=pl.ANY),
        out_shape=jax.ShapeDtypeStruct((16 * ROWS, sources[0].shape[1]), BF16),
        scratch_shapes=[pltpu.SemaphoreType.DMA((16,))],
        compiler_params=pltpu.CompilerParams(vmem_limit_bytes=2**20),
        cost_estimate=SMALL,
        name="place_rows",
    )(slots, *sources)


def scale_kernel(slots, *refs):
    blocks, product, out_ref = refs[:16], refs[16], refs[17]
    total = jnp.zeros(out_ref.shape, F32)
    for at, block in enumerate(blocks):
        row = pl.multiple_of(slots[at] * ROWS, ROWS)
        for tile in range(0, ROWS, 16):
            left = block[pl.ds(tile, 16), :].astype(F32)
            right = product[pl.ds(row + tile, 16), :].astype(F32)
            term = left * right
            total = total + term[:8] + term[8:]
    out_ref[...] = total


def scale_sum(slots, blocks, product):
    width = product.shape[1]
    cols = 1024
    return pl.pallas_call(
        scale_kernel,
        grid_spec=pltpu.PrefetchScalarGridSpec(
            num_scalar_prefetch=1,
            grid=(width // cols,),
            in_specs=[pl.BlockSpec((v.shape[0], cols), lambda j, o: (0, j)) for v in (*blocks, product)],
            out_specs=pl.BlockSpec((8, cols), lambda j, o: (0, j)),
        ),
        out_shape=jax.ShapeDtypeStruct((8, width), F32),
        compiler_params=pltpu.CompilerParams(vmem_limit_bytes=60 * 2**20),
        cost_estimate=SMALL,
        name="scale_sum",
    )(slots, *blocks, product)


def on_device(inputs, gain, w_in, grad_act, residual_gradient):
    dp_index = lax.axis_index("dp")
    t_index = lax.axis_index("tensor")
    x_at, yh_at, c_at = dp_index // 4, (dp_index // 2) % 2, dp_index % 2
    y_at, z_at = t_index // NZ, t_index % NZ

    with jax.named_scope("norm"):
        values = inputs.astype(F32)
        centered_input = values - jnp.mean(values, axis=1, keepdims=True)
        inverse_deviation = lax.rsqrt(
            jnp.mean(centered_input * centered_input, axis=1, keepdims=True) + 1e-06
        )
        standardized_input = centered_input * inverse_deviation
        normed_output = (standardized_input * gain).astype(BF16)

    def slots(keys):
        places = [
            (y_at if column == "A" else 1 - y_at) * NZ + (z_at + offset) % NZ for column, offset in keys
        ]
        return jnp.stack(places).astype(jnp.int32)

    place = jnp.stack([yh_at, c_at]).astype(jnp.int32)
    order = jnp.stack([(x_at + k) % 4 for k in (2, 1, 3, 0)]).astype(jnp.int32)
    got = {("A", 0): normed_output}
    rights = []

    def dense(at):
        rights.append(forward(slots(GROUPS[at]), [got[key] for key in GROUPS[at]], w_in, grad_act))

    with jax.named_scope("gather"):
        for at, moves in enumerate(MOVES):
            for key, move, source in moves:
                got[key] = move(got[source])
            if at == 2:
                got["A", 3], order, place = together(got["A", 3], order, place)
            along_z = [key for key, move, _ in moves if move is not swap_y]
            held = [got[key] for key in along_z]
            if at >= 1:
                dense(at - 1)
                held.append(rights[-1])
            later = [source for _, move, source in MOVES[at + 1] if move is swap_y] if at < 4 else []
            held = list(together(*held, *[got[key] for key in later if key not in along_z]))
            for key in along_z:
                got[key] = held.pop(0)
            for key in later:
                if key not in along_z:
                    got[key] = held.pop()
            if at >= 1:
                rights[-1] = held.pop(0)

    with jax.named_scope("turn"):
        dense(4)
        blocks = [got[key] for keys in GROUPS for key in keys]
        rows = slots([key for keys in GROUPS for key in keys])
        product = backward(place_rows(rows, rights), w_in)

    with jax.named_scope("scatter"):
        normed_gradient = lax.psum_scatter(product, "tensor", scatter_dimension=0, tiled=True).astype(F32)

    half = w_in.shape[1] // 2

    def hop(total, axis, bit):
        return total + ppermute(total, axis, lambda i: i ^ bit)

    def moving(mine, theirs, far, chunk, way):
        first = add(mine[chunk, :half], theirs[chunk, :half], *([far[0]] if way > 0 else []))
        second = add(mine[chunk, half:], theirs[chunk, half:], *([far[0]] if way < 0 else []))
        return jnp.concatenate([first, second], 0)

    with jax.named_scope("weights"):
        first, second = together(order[:1], order[1:], product[:1, :1])[:2]
        far_mine, far_theirs = weight_terms(first, place, blocks, rights)
        sums = scale_sum(rows, blocks, product)
        total = jnp.sum(sums, axis=0).reshape(48, 128)
        far_mine, far_theirs, second, total = together(far_mine, far_theirs, second, total)
        mine, theirs = weight_terms(second, place, blocks, rights)
        total = hop(hop(total, "dp", 1), "dp", 4)
        far_mine, far_theirs, mine, theirs, total = together(far_mine, far_theirs, mine, theirs, total)

    with jax.named_scope("core_far"):
        (swapped,) = together(swap_core(far_theirs))
        far, theirs, total = together(add(far_mine, swapped), theirs, total)

    with jax.named_scope("x_far"):
        far_up, far_down = to_x(far[:, :half], 1), to_x(far[:, half:], -1)
        theirs = swap_core(theirs)
        total = hop(total, "dp", 2)
        far_up, far_down, theirs, total = together(far_up, far_down, theirs, total)

    with jax.named_scope("x_other"):
        up_other, down_other = moving(mine, theirs, far_up[:1], 0, 1), moving(mine, theirs, far_down[:1], 2, -1)
        up_other, down_other, total = together(up_other, down_other, total)
        up_moved, down_moved = to_x(up_other, 1), to_x(down_other, -1)
        up_own, down_own = moving(mine, theirs, far_up[1:], 1, 1), moving(mine, theirs, far_down[1:], 3, -1)
        total = hop(hop(hop(total, "tensor", 1), "tensor", 2), "tensor", 4)
        up_moved, down_moved, up_own, down_own, total = together(
            up_moved, down_moved, up_own, down_own, total
        )

    with jax.named_scope("x_own"):
        other = add(mine[4], theirs[4], up_moved, down_moved)
        up_own, down_own, other, total = together(up_own, down_own, other, total)
        from_y = swap_yh(other)
        up_moved, down_moved = to_x(up_own, 1), to_x(down_own, -1)
        own = mine[5].astype(F32) + theirs[5].astype(F32)
        for value in (up_moved, down_moved, from_y):
            own = own + value.astype(F32)
        grad_w = (own / 16).T
        total = together(total, normed_gradient[:1, :1])[0]
        last = ppermute(total, "dp", lambda i: i ^ 8)

    with jax.named_scope("input_gradient"):
        scaled_gradient = normed_gradient * gain
        first_average = jnp.mean(scaled_gradient, axis=1, keepdims=True)
        second_average = jnp.mean(scaled_gradient * standardized_input, axis=1, keepdims=True)
        block_input_gradient = (
            residual_gradient.astype(F32)
            + inverse_deviation
            * (scaled_gradient - first_average - standardized_input * second_average)
        ).astype(BF16)
    with jax.named_scope("scale_gradient"):
        last, block_input_gradient = together(last, block_input_gradient)
        scale_gradient = hop(total + last, "tensor", 8).reshape(-1) / gain / 16
    return (block_input_gradient, grad_w, scale_gradient)


def solution(mesh):
    return jax.shard_map(
        on_device,
        mesh=mesh,
        in_specs=(
            P(("dp", "tensor"), None),
            P(),
            P(None, "tensor"),
            P("dp", "tensor"),
            P(("dp", "tensor"), None),
        ),
        out_specs=(P(("dp", "tensor"), None), P("dp", "tensor"), P()),
        check_vma=False,
    )
```
